128 devices in a mesh: row: 8 (over y_lo, x), col: 16 (over y_hi, z, core).
Axes of the slice: x: 4, y: 4 (y_hi: 2, y_lo: 2; y = y_hi * 2 + y_lo), z: 4, core: 2. Of those that a mesh axis runs over, the one named last changes fastest.
Arguments:
- inputs: bfloat16 [1024, 12288], P('row', 'col'), may hold values from -6 to 6
- grad_out: bfloat16 [1024, 12288], P('row', 'col'), may hold values from -1 to 1
- w_in: bfloat16 [12288, 24576], P('col', 'row'), may hold values from -0.0546875 to 0.0546875
- bias_in: float32 [24576], P('row'), may hold values from -3 to 3
- w_out: bfloat16 [24576, 12288], P('row', 'col'), may hold values from -0.0546875 to 0.0546875
Outputs:
- grad_in: bfloat16 [1024, 12288], P('row', 'col')
- grad_w_in: bfloat16 [12288, 24576], P('col', 'row')
- grad_w_out: bfloat16 [24576, 12288], P('row', 'col')
- grad_bias: float32 [24576], P(('row', 'col'))
The draws below stay inside these ranges and needn't reach their ends.
All inputs are finite; a program needn't handle non-finite values.
Results may differ from the reference program's by a relative error of at most 0.035.
Values may be sent and summed in bfloat16 or wider, within the bound.
No kernel may reach another device: no remote copies, remote signals or barrier semaphores. Data moves between devices by JAX's collectives and lax.ppermute only.
A program may use at most 128 MiB of HBM per device.

```python
import jax
import jax.numpy as jnp
from jax import lax

D = 12288
FFN = 24576
TOKENS = 1024
N_COL = 16


def with_spikes(drawn, stream_key, source, target, shards_of, factor):
    def block_of(dim):
        return (jnp.arange(drawn.shape[dim]) // (drawn.shape[dim] // shards_of)).reshape((-1,) + (1,) * (drawn.ndim - 1 - dim))

    near = jax.random.permutation(stream_key, shards_of)[block_of(target)]
    second = (block_of(target) + shards_of // 2) % shards_of
    return jnp.where((block_of(source) == near) | (block_of(source) == second), factor * drawn, drawn)


def levels(key, shape, shards, low, top_value):
    gain = 1.0
    for axis_at, shards_of in shards:
        draws = jax.random.uniform(jax.random.fold_in(jax.random.fold_in(key, 6), axis_at), (shards_of,), jnp.float32, low / len(shards), top_value / len(shards))
        gain = gain * jnp.repeat(jnp.exp(draws), shape[axis_at] // shards_of).reshape((-1,) + (1,) * (len(shape) - 1 - axis_at))
    return gain


def bell_draw(stream_key, dims, deviation, bound, cuts=(), held_as=jnp.bfloat16):
    level = levels(stream_key, dims, cuts, -0.22, 0.18) if cuts else 1.0
    array = jax.random.normal(stream_key, dims, jnp.float32) * deviation * level
    return jnp.minimum(jnp.maximum(array, -bound), bound).astype(held_as)


def gaussian_with(own_key, shape, scale, limit, pieces, heavy, kind=jnp.bfloat16):
    array = scale * jax.random.normal(own_key, shape, jnp.float32)
    if pieces:
        array = array * levels(own_key, shape, pieces, -0.22, 0.18)
    return jnp.clip(with_spikes(array, jax.random.fold_in(own_key, 3), *heavy), -limit, limit).astype(kind)


def setup_inputs(seed: int = 0) -> dict:
    seeds = jax.random.split(jax.random.key(seed), 6)
    return {
        "inputs": gaussian_with(seeds[0], (TOKENS, D), 1.0, 6.0, ((0, 8), (1, 16)), (1, 0, 16, 2.0)),
        "grad_out": gaussian_with(seeds[1], (TOKENS, D), 0.125, 1.0, ((0, 8), (1, 16)), (1, 0, 16, 2.0)),
        "w_in": bell_draw(seeds[2], (D, FFN), D ** -0.5, 0.0546875, ((0, 16), (1, 8))),
        "bias_in": bell_draw(seeds[3], (FFN,), 0.5, 3.0, ((0, 8),), jnp.float32),
        "w_out": bell_draw(seeds[4], (FFN, D), D ** -0.5, 0.0546875, ((0, 8), (1, 16))),
    }


coeff = 0.7978845608028654


def gelu_pair(preact, grad_act, bias):
    shifted = preact + bias[None, :]
    tangent = jnp.tanh(coeff * (shifted + 0.044715 * shifted * shifted * shifted))
    activated = 0.5 * shifted * (1.0 + tangent)
    slope = 0.5 * (1.0 + tangent) + 0.5 * shifted * (1.0 - tangent * tangent) * coeff * (1.0 + 3.0 * 0.044715 * shifted * shifted)
    return activated.astype(jnp.bfloat16), (grad_act * slope).astype(jnp.bfloat16)


def rounded(value):
    return lax.optimization_barrier(value.astype(jnp.bfloat16)).astype(jnp.float32)


def reference(inputs, grad_out, w_in, bias_in, w_out):
    columns = D // N_COL
    tokens = inputs.shape[0]
    hidden = w_in.shape[1]

    def accumulate(totals, block):
        offset = (block * columns).astype(jnp.int32)
        x_block = lax.dynamic_slice_in_dim(inputs, offset, columns, 1)
        y_block = lax.dynamic_slice_in_dim(grad_out, offset, columns, 1)
        w_block = lax.dynamic_slice_in_dim(w_in, offset, columns, 0)
        v_block = lax.dynamic_slice_in_dim(w_out, offset, columns, 1)
        pre_term = jnp.dot(x_block, w_block, preferred_element_type=jnp.float32)
        act_term = lax.dot_general(y_block, v_block, (((1,), (1,)), ((), ())), preferred_element_type=jnp.float32)
        return (totals[0] + rounded(pre_term), totals[1] + rounded(act_term)), None

    start_sums = (jnp.zeros((tokens, hidden), jnp.float32), jnp.zeros((tokens, hidden), jnp.float32))
    (preact, grad_act), _ = lax.scan(accumulate, start_sums, jnp.arange(N_COL, dtype=jnp.int32))
    activated, grad_pre = gelu_pair(preact, grad_act, bias_in.astype(jnp.float32))
    grad_w_out = lax.dot_general(activated, grad_out, (((0,), (0,)), ((), ())), preferred_element_type=jnp.float32).astype(jnp.bfloat16)
    grad_w_in = lax.dot_general(inputs, grad_pre, (((0,), (0,)), ((), ())), preferred_element_type=jnp.float32).astype(jnp.bfloat16)
    grad_bias = jnp.sum(grad_pre.astype(jnp.float32), axis=0)
    grad_in = lax.dot_general(grad_pre, w_in, (((1,), (1,)), ((), ())), preferred_element_type=jnp.float32).astype(jnp.bfloat16)
    return grad_in, grad_w_in, grad_w_out, grad_bias
```

```python
import jax
import jax.numpy as jnp
from jax import lax
from jax.sharding import PartitionSpec as P

coeff = 0.7978845608028654
AXES = ("row", "col")
F32, BF16 = jnp.float32, jnp.bfloat16


def place(y, x, z, core):
    y, x, z = y % 4, x % 4, z % 4
    return ((y % 2) * 4 + x) * 16 + ((y // 2) * 4 + z) * 2 + core


def shift(value, dx=0, dz=0, pair=False, far=False, swap=False):
    table = []
    for y in range(4):
        for x in range(4):
            for z in range(4):
                for k in range(2):
                    to_y = y ^ 1 if pair else y + 2 if far else y
                    table.append((place(y, x, z, k), place(to_y, x + dx, z + dz, k ^ 1 if swap else k)))
    return lax.ppermute(value, AXES, table)


def gelu_pair(preact, grad_act, bias):
    shifted = preact + bias
    tangent = jnp.tanh(coeff * (shifted + 0.044715 * shifted * shifted * shifted))
    activated = 0.5 * shifted * (1.0 + tangent)
    slope = 0.5 * (1.0 + tangent) + 0.5 * shifted * (1.0 - tangent * tangent) * coeff * (
        1.0 + 3.0 * 0.044715 * shifted * shifted
    )
    return activated.astype(BF16), (grad_act * slope).astype(BF16)


def contract(left, right, left_dim, right_dim):
    return lax.dot_general(left, right, (((left_dim,), (right_dim,)), ((), ())), preferred_element_type=F32)


def add(*terms):
    return sum(t.astype(F32) for t in terms).astype(BF16)


def relative_rows():
    col = lax.axis_index("col")
    core, z, y_hi = col % 2, (col // 2) % 4, col // 8
    row = jnp.arange(128, dtype=jnp.int32)[:, None]
    slot = row // 8
    d_core, d_z, d_y = slot // 8, (slot // 2) % 4, slot % 2
    d_z = jnp.where(d_z == 2, 3, jnp.where(d_z == 3, 2, d_z))
    source = ((jnp.bitwise_xor(y_hi, d_y) * 4 + (z + d_z) % 4) * 2 + jnp.bitwise_xor(core, d_core)) * 8 + row % 8
    return (source == jnp.arange(128, dtype=jnp.int32)[None, :]).astype(BF16)


def ring_of_rows(block):
    plus, minus = shift(block, dx=-1), shift(block, dx=1)
    far = jnp.stack([shift(minus[0], dx=1), shift(plus[1], dx=-1)])
    return plus, minus, far


def partial_sums(pieces, w_in, w_out):
    m = len(pieces)
    rows = [p.reshape(2, 2, 64, -1) for p in pieces]

    def both(core):
        x = jnp.concatenate([r[0, core] for r in rows])
        g = jnp.concatenate([r[1, core] for r in rows])
        return jnp.stack([contract(x, w_in, 1, 0).astype(BF16), contract(g, w_out, 1, 1).astype(BF16)])

    sent = both(1)
    got = shift(sent, swap=True)
    kept = both(0)
    return add(kept, got).reshape(2, m, 4, 2, 8, -1)


def z_first(q):
    via_plus = shift(q[:, :, 3, 0], dz=1)
    via_minus = shift(q[:, :, 3, 1], dz=-1)
    plus = jnp.stack([add(q[:, :, 1, 0], via_plus), q[:, :, 1, 1]], axis=2)
    minus = jnp.stack([q[:, :, 2, 0], add(q[:, :, 2, 1], via_minus)], axis=2)
    from_minus, from_plus = shift(plus, dz=1), shift(minus, dz=-1)
    total = sum(t.astype(F32) for t in (q[:, :, 0], from_minus, from_plus))
    got = shift(total[:, :, 1].astype(BF16), far=True)
    return total[:, :, 0] + got.astype(F32)


def y_first(q):
    got = shift(q[:, :, :, 1], far=True)
    r = add(q[:, :, :, 0], got)
    via_plus = shift(r[0, :, 3], dz=1)
    via_minus = shift(r[1, :, 3], dz=-1)
    plus = jnp.stack([add(r[0, :, 1], via_plus), r[1, :, 1]])
    minus = jnp.stack([r[0, :, 2], add(r[1, :, 2], via_minus)])
    from_minus, from_plus = shift(plus, dz=1), shift(minus, dz=-1)
    return sum(t.astype(F32) for t in (r[:, :, 0], from_minus, from_plus))


def y_then_z(u):
    u = jnp.stack([u, shift(u, far=True)], axis=2)
    minus, plus = shift(u, dz=1), shift(u, dz=-1)
    far = jnp.stack([shift(minus[:, :, 0], dz=1), shift(plus[:, :, 1], dz=-1)], axis=2)
    return jnp.stack([u, plus, minus, far], axis=2)


def z_then_y(u):
    minus, plus = shift(u, dz=1), shift(u, dz=-1)
    far = jnp.stack([shift(minus[0], dz=1), shift(plus[1], dz=-1)])
    v = jnp.stack([u, plus, minus, far], axis=2)
    return jnp.stack([v, shift(v, far=True)], axis=3)


def local(inputs, grad_out, w_in, bias_in, w_out):
    hidden = w_in.shape[1]
    order = relative_rows()
    own = jnp.stack([contract(order, a, 1, 0).astype(BF16) for a in (inputs, grad_out)])
    other = shift(own, pair=True)
    near, beside = ring_of_rows(own), ring_of_rows(other)
    groups = [[own, *near, other], list(beside)]
    sums = [partial_sums(p, w_in, w_out) for p in groups]
    totals = [z_first(sums[0]), y_first(sums[1])]
    shards = [jnp.stack(gelu_pair(t[0], t[1], bias_in)) for t in totals]
    halves = [y_then_z(shards[0]), z_then_y(shards[1])]
    rows_act, rows_pre, rows_x, rows_g = [], [], [], []
    for half, pieces in zip(halves, groups):
        split = [p.reshape(2, 2, 64, -1) for p in pieces]
        for core, v in enumerate((half, shift(half, swap=True))):
            v = v.reshape(2, -1, hidden)
            rows_act.append(v[0])
            rows_pre.append(v[1])
            rows_x += [s[0, core] for s in split]
            rows_g += [s[1, core] for s in split]
    act, pre = jnp.concatenate(rows_act), jnp.concatenate(rows_pre)
    x_all, g_all = jnp.concatenate(rows_x), jnp.concatenate(rows_g)
    back = contract(pre, w_in, 1, 1).astype(BF16)
    by_owner, at = [], 0
    for pieces in groups:
        m = len(pieces)
        part = back[at : at + m * 128].reshape(2, m, 64, -1)
        by_owner += [part[:, i].reshape(128, -1) for i in range(m)]
        at += m * 128
    own_b, plus_b, minus_b, far_b, other_b, oplus_b, ominus_b, ofar_b = by_owner
    mine = jnp.stack([own_b, other_b])
    to_plus, to_minus, to_far = jnp.stack([plus_b, oplus_b]), jnp.stack([minus_b, ominus_b]), jnp.stack([far_b, ofar_b])
    via_plus, via_minus = shift(to_far[0], dx=1), shift(to_far[1], dx=-1)
    to_plus = jnp.stack([add(to_plus[0], via_plus), to_plus[1]])
    to_minus = jnp.stack([to_minus[0], add(to_minus[1], via_minus)])
    total = sum(t.astype(F32) for t in (mine, shift(to_plus, dx=1), shift(to_minus, dx=-1)))
    total = total[0] + shift(total[1].astype(BF16), pair=True).astype(F32)
    grad_in = contract(order, total.astype(BF16), 0, 0).astype(BF16)
    grad_w_out = contract(act, g_all, 0, 0).astype(BF16)
    grad_w_in = contract(x_all, pre, 0, 0).astype(BF16)
    bias_sum = jnp.sum(pre.astype(F32), axis=0)
    portion = hidden // lax.axis_size("col")
    grad_bias = lax.dynamic_slice_in_dim(bias_sum, lax.axis_index("col") * portion, portion, 0)
    return grad_in, grad_w_in, grad_w_out, grad_bias


def solution(mesh):
    return jax.shard_map(
        local,
        mesh=mesh,
        in_specs=(P("row", "col"), P("row", "col"), P("col", "row"), P("row"), P("row", "col")),
        out_specs=(P("row", "col"), P("col", "row"), P("row", "col"), P(("row", "col"))),
        check_vma=False,
    )
```

```python
import jax
import jax.numpy as jnp
from jax import lax
from jax.sharding import PartitionSpec as P

coeff = 0.7978845608028654
AXES = ("row", "col")
F32, BF16 = jnp.float32, jnp.bfloat16


def place(y, x, z, core):
    y, x, z = y % 4, x % 4, z % 4
    return ((y % 2) * 4 + x) * 16 + ((y // 2) * 4 + z) * 2 + core


def shift(value, dx=0, dz=0, pair=False, far=False, swap=False):
    table = []
    for y in range(4):
        for x in range(4):
            for z in range(4):
                for k in range(2):
                    to_y = y ^ 1 if pair else y + 2 if far else y
                    table.append((place(y, x, z, k), place(to_y, x + dx, z + dz, k ^ 1 if swap else k)))
    return lax.ppermute(value, AXES, table)


def gelu_pair(preact, grad_act, bias):
    shifted = preact + bias
    tangent = jnp.tanh(coeff * (shifted + 0.044715 * shifted * shifted * shifted))
    activated = 0.5 * shifted * (1.0 + tangent)
    slope = 0.5 * (1.0 + tangent) + 0.5 * shifted * (1.0 - tangent * tangent) * coeff * (
        1.0 + 3.0 * 0.044715 * shifted * shifted
    )
    return activated.astype(BF16), (grad_act * slope).astype(BF16)


def contract(left, right, left_dim, right_dim):
    return lax.dot_general(left, right, (((left_dim,), (right_dim,)), ((), ())), preferred_element_type=F32)


def add(*terms):
    return sum(t.astype(F32) for t in terms).astype(BF16)


def relative_rows():
    col = lax.axis_index("col")
    core, z, y_hi = col % 2, (col // 2) % 4, col // 8
    row = jnp.arange(128, dtype=jnp.int32)[:, None]
    slot = row // 8
    d_core, d_z, d_y = slot // 8, (slot // 2) % 4, slot % 2
    d_z = jnp.where(d_z == 2, 3, jnp.where(d_z == 3, 2, d_z))
    source = ((jnp.bitwise_xor(y_hi, d_y) * 4 + (z + d_z) % 4) * 2 + jnp.bitwise_xor(core, d_core)) * 8 + row % 8
    return (source == jnp.arange(128, dtype=jnp.int32)[None, :]).astype(BF16)


def after(value, *earlier):
    return lax.optimization_barrier((value, *earlier))[0]


def total(*terms):
    return sum(t.astype(F32) for t in terms)


def swapped(value):
    return shift(value, swap=True)


def local(inputs, grad_out, w_in, bias_in, w_out):
    hidden = w_in.shape[1]
    order = relative_rows()

    own = jnp.stack([contract(order, a, 1, 0).astype(BF16) for a in (inputs, grad_out)])
    plus, minus, other = shift(own, dx=-1), shift(own, dx=1), shift(own, pair=True)
    far = jnp.stack([shift(minus[0], dx=1), shift(plus[1], dx=-1)])
    other_plus, other_minus = shift(other, dx=-1), shift(other, dx=1)
    other_far = shift(far, pair=True)
    pieces_a = [own, plus, minus, far, other]
    pieces_b = [other_plus, other_minus, other_far]

    def rows(pieces, array, core):
        return jnp.concatenate([p.reshape(2, 2, 64, -1)[array, core] for p in pieces])

    def pair_sums(pieces):
        m = len(pieces)
        sums = []
        for i, w, dim in ((0, w_in, 0), (1, w_out, 1)):
            both = contract(jnp.concatenate([rows(pieces, i, 0), rows(pieces, i, 1)]), w, 1, dim).astype(BF16)
            got = swapped(both[m * 64 :])
            sums.append((both[: m * 64].reshape(m, 4, 2, 8, hidden), got.reshape(m, 4, 2, 8, hidden)))
        return sums

    def pick(sums, *at):
        return jnp.stack([add(k[(slice(None), *at)], g[(slice(None), *at)]) for k, g in sums])

    def pick_f32(sums, *at):
        return jnp.stack([total(k[(slice(None), *at)], g[(slice(None), *at)]) for k, g in sums])

    a = pair_sums(pieces_a)
    a_far0, a_far1 = pick(a, 3, 0), pick(a, 3, 1)
    a_via_plus, a_via_minus = shift(a_far0, dz=1), shift(a_far1, dz=-1)
    pieces_b = list(lax.optimization_barrier((*pieces_b, a_far0, a_far1))[:3])
    b = pair_sums(pieces_b)
    a_plus = jnp.stack([add(pick_f32(a, 1, 0), a_via_plus), pick(a, 1, 1)])
    a_minus = jnp.stack([pick(a, 2, 0), add(pick_f32(a, 2, 1), a_via_minus)])
    a_from_minus, a_from_plus = shift(a_plus, dz=1), shift(a_minus, dz=-1)
    b_got = shift(after(pick(b, slice(None), 1), a_via_plus, a_via_minus), far=True)
    a_half = [total(pick_f32(a, 0, y), a_from_minus[y], a_from_plus[y]) for y in (0, 1)]
    a_sent = a_half[1].astype(BF16)
    a_got = shift(a_sent, far=True)
    b_got = after(b_got, a_sent)
    b_sum = [total(pick_f32(b, z, 0), b_got[:, :, z]) for z in range(4)]
    b_far0, b_far1 = b_sum[3][0].astype(BF16), b_sum[3][1].astype(BF16)
    b_via_plus, b_via_minus = shift(b_far0, dz=1), shift(b_far1, dz=-1)
    b_plus = jnp.stack([add(b_sum[1][0], b_via_plus), b_sum[1][1].astype(BF16)])
    b_minus = jnp.stack([b_sum[2][0].astype(BF16), add(b_sum[2][1], b_via_minus)])
    b_from_minus, b_from_plus = shift(b_plus, dz=1), shift(b_minus, dz=-1)
    a_got = after(a_got, b_plus, b_minus)

    def shard(t):
        return tuple(v.reshape(-1, hidden) for v in gelu_pair(t[0], t[1], bias_in))

    ua = shard(total(a_half[0], a_got))
    ub = shard(total(b_sum[0], b_from_minus, b_from_plus))
    na, nb = ua[0].shape[0], ub[0].shape[0]

    def packed(*blocks):
        return jnp.concatenate(blocks)

    def opened(value, *sizes):
        ends, at = [], 0
        for n in sizes[:-1]:
            at += n
            ends.append(at)
        return jnp.split(value, ends)

    four = (na, na, nb, nb)
    u = packed(*ua, *ub)
    held = lax.optimization_barrier((*pieces_a, *pieces_b, u))
    pieces_a, pieces_b, u = held[:5], held[5:8], held[8]
    minus1, plus1, y1 = shift(u, dz=1), shift(u, dz=-1), shift(u, far=True)
    ma0, ma1, mb0, mb1 = opened(minus1, *four)
    pa0, pa1, pb0, pb1 = opened(plus1, *four)
    ya0, ya1, yb0, yb1 = opened(y1, *four)
    minus2 = shift(packed(ya0, ya1, ma0, mb0), dz=1)
    plus2 = shift(packed(ya0, ya1, pa1, pb1), dz=-1)
    y2 = shift(packed(pb0, pb1, mb0, mb1), far=True)
    mya0, mya1, fa0, fb0 = opened(minus2, na, na, na, nb)
    pya0, pya1, fa1, fb1 = opened(plus2, na, na, na, nb)
    ypb0, ypb1, ymb0, ymb1 = opened(y2, nb, nb, nb, nb)
    minus3, plus3 = shift(mya0, dz=1), shift(pya1, dz=-1)
    y3 = shift(packed(fb0, fb1), far=True)

    early = [
        (*ua, 0, 0, 0), (*ub, 1, 0, 0),
        (ma0, ma1, 0, 2, 0), (mb0, mb1, 1, 2, 0), (pa0, pa1, 0, 1, 0), (pb0, pb1, 1, 1, 0),
        (ya0, ya1, 0, 0, 1), (yb0, yb1, 1, 0, 1),
        (mya0, mya1, 0, 2, 1), (pya0, pya1, 0, 1, 1), (fa0, fa1, 0, 3, 0), (fb0, fb1, 1, 3, 0),
        (ypb0, ypb1, 1, 1, 1), (ymb0, ymb1, 1, 2, 1),
    ]
    late = [(minus3, plus3, 0, 3, 1), (*opened(y3, nb, nb), 1, 3, 1)]

    def both_cores(*rounds):
        act, pre = [], []
        for blocks in rounds:
            act.append(packed(*[b[0] for b in blocks]))
            pre.append(packed(*[b[1] for b in blocks]))
        swap = [swapped(packed(a, p)) for a, p in zip(act, pre)]
        act += [s[: s.shape[0] // 2] for s in swap]
        pre += [s[s.shape[0] // 2 :] for s in swap]
        return packed(*act), packed(*pre)

    act_early, pre_early = both_cores(early[:2], early[2:8], early[8:])
    act_late, pre_late = both_cores(late)
    places_early, places_late = ([(core, *b[2:]) for core in (0, 1) for b in part] for part in (early, late))

    def matching(array):
        parts = [jnp.stack([p[array].reshape(2, 4, 2, 8, -1) for p in pieces]) for pieces in (pieces_a, pieces_b)]
        return jnp.concatenate([parts[n][:, c, z, y].reshape(-1, parts[n].shape[-1]) for c, n, z, y in places_early + places_late])

    x_all, g_all = matching(0), matching(1)
    back = packed(contract(pre_early, w_in, 1, 1).astype(BF16), contract(pre_late, w_in, 1, 1).astype(BF16))
    found, at = {}, 0
    for place_of in places_early + places_late:
        n = (na, nb)[place_of[1]]
        found[place_of] = back[at : at + n].reshape(n // 8, 8, -1)
        at += n
    by_owner = []
    for part in (0, 1):
        slots = [found[core, part, z, y] for core in (0, 1) for z in range(4) for y in (0, 1)]
        v = jnp.stack(slots, axis=1)
        by_owner += [v[i].reshape(128, -1) for i in range(v.shape[0])]
    own_b, plus_b, minus_b, far_b, other_b, oplus_b, ominus_b, ofar_b = by_owner
    row = lax.axis_index("row")
    here = jnp.stack([own_b, plus_b, far_b, minus_b])
    there = jnp.stack([other_b, oplus_b, ofar_b, ominus_b])
    upper = row >= 4
    planes = (jnp.where(upper, there, here), jnp.where(upper, here, there))
    x_at = (4 - row % 4) % 4
    turned = [lax.dynamic_slice_in_dim(jnp.concatenate([p, p]), x_at, 4, 0) for p in planes]
    arrived = lax.all_to_all(jnp.concatenate(turned), "row", split_axis=0, concat_axis=0, tiled=True)
    act, pre = packed(act_early, act_late), packed(pre_early, pre_late)
    grad_w_out = contract(act, g_all, 0, 0).astype(BF16)
    grad_w_in = contract(x_all, pre, 0, 0).astype(BF16)
    bias_sum = jnp.sum(pre.astype(F32), axis=0)
    portion = hidden // lax.axis_size("col")
    grad_bias = lax.dynamic_slice_in_dim(bias_sum, lax.axis_index("col") * portion, portion, 0)
    grad_in = contract(order, arrived.astype(F32).sum(axis=0).astype(BF16), 0, 0).astype(BF16)
    return grad_in, grad_w_in, grad_w_out, grad_bias


def solution(mesh):
    return jax.shard_map(
        local,
        mesh=mesh,
        in_specs=(P("row", "col"), P("row", "col"), P("col", "row"), P("row"), P("row", "col")),
        out_specs=(P("row", "col"), P("col", "row"), P("row", "col"), P(("row", "col"))),
        check_vma=False,
    )
```

```python
import jax
import jax.numpy as jnp
from jax import lax
from jax.sharding import PartitionSpec as P

coeff = 0.7978845608028654
AXES = ("row", "col")
F32, BF16 = jnp.float32, jnp.bfloat16


def place(y, x, z, core):
    y, x, z = y % 4, x % 4, z % 4
    return ((y % 2) * 4 + x) * 16 + ((y // 2) * 4 + z) * 2 + core


def shift(value, dx=0, dz=0, pair=False, far=False, swap=False):
    table = []
    for y in range(4):
        for x in range(4):
            for z in range(4):
                for k in range(2):
                    to_y = y ^ 1 if pair else y + 2 if far else y
                    table.append((place(y, x, z, k), place(to_y, x + dx, z + dz, k ^ 1 if swap else k)))
    return lax.ppermute(value, AXES, table)


def gelu_pair(preact, grad_act, bias):
    shifted = preact + bias
    tangent = jnp.tanh(coeff * (shifted + 0.044715 * shifted * shifted * shifted))
    activated = 0.5 * shifted * (1.0 + tangent)
    slope = 0.5 * (1.0 + tangent) + 0.5 * shifted * (1.0 - tangent * tangent) * coeff * (
        1.0 + 3.0 * 0.044715 * shifted * shifted
    )
    return activated.astype(BF16), (grad_act * slope).astype(BF16)


def contract(left, right, left_dim, right_dim):
    return lax.dot_general(left, right, (((left_dim,), (right_dim,)), ((), ())), preferred_element_type=F32)


def add(*terms):
    return sum(t.astype(F32) for t in terms).astype(BF16)


def relative_rows():
    col = lax.axis_index("col")
    core, z, y_hi = col % 2, (col // 2) % 4, col // 8
    row = jnp.arange(128, dtype=jnp.int32)[:, None]
    slot = row // 8
    d_core, d_z, d_y = slot // 8, (slot // 2) % 4, slot % 2
    d_z = jnp.where(d_z == 2, 3, jnp.where(d_z == 3, 2, d_z))
    source = ((jnp.bitwise_xor(y_hi, d_y) * 4 + (z + d_z) % 4) * 2 + jnp.bitwise_xor(core, d_core)) * 8 + row % 8
    return (source == jnp.arange(128, dtype=jnp.int32)[None, :]).astype(BF16)


def after(value, *earlier):
    return lax.optimization_barrier((value, *earlier))[0]


def total(*terms):
    return sum(t.astype(F32) for t in terms)


def swapped(value):
    return shift(value, swap=True)


def local(inputs, grad_out, w_in, bias_in, w_out):
    hidden = w_in.shape[1]
    order = relative_rows()

    own = jnp.stack([contract(order, a, 1, 0).astype(BF16) for a in (inputs, grad_out)])
    plus, minus, other = shift(own, dx=-1), shift(own, dx=1), shift(own, pair=True)
    far = jnp.stack([shift(minus[0], dx=1), shift(plus[1], dx=-1)])
    other_plus, other_minus = shift(other, dx=-1), shift(other, dx=1)
    other_far = shift(far, pair=True)
    pieces_a = [own, plus, minus, far, other]
    pieces_b = [other_plus, other_minus, other_far]

    def rows(pieces, array, core):
        return jnp.concatenate([p.reshape(2, 2, 64, -1)[array, core] for p in pieces])

    def pair_sums(pieces):
        m = len(pieces)
        sums = []
        for i, w, dim in ((0, w_in, 0), (1, w_out, 1)):
            both = contract(jnp.concatenate([rows(pieces, i, 0), rows(pieces, i, 1)]), w, 1, dim).astype(BF16)
            got = swapped(both[m * 64 :])
            sums.append((both[: m * 64].reshape(m, 4, 2, 8, hidden), got.reshape(m, 4, 2, 8, hidden)))
        return sums

    def pick(sums, *at):
        return jnp.stack([add(k[(slice(None), *at)], g[(slice(None), *at)]) for k, g in sums])

    def pick_f32(sums, *at):
        return jnp.stack([total(k[(slice(None), *at)], g[(slice(None), *at)]) for k, g in sums])

    a = pair_sums(pieces_a)
    a_far0, a_far1 = pick(a, 3, 0), pick(a, 3, 1)
    a_via_plus, a_via_minus = shift(a_far0, dz=1), shift(a_far1, dz=-1)
    pieces_b = list(lax.optimization_barrier((*pieces_b, a_far0, a_far1))[:3])
    b = pair_sums(pieces_b)
    a_plus = jnp.stack([add(pick_f32(a, 1, 0), a_via_plus), pick(a, 1, 1)])
    a_minus = jnp.stack([pick(a, 2, 0), add(pick_f32(a, 2, 1), a_via_minus)])
    a_from_minus, a_from_plus = shift(a_plus, dz=1), shift(a_minus, dz=-1)
    b_got = shift(after(pick(b, slice(None), 1), a_via_plus, a_via_minus), far=True)
    a_half = [total(pick_f32(a, 0, y), a_from_minus[y], a_from_plus[y]) for y in (0, 1)]
    a_sent = a_half[1].astype(BF16)
    a_got = shift(a_sent, far=True)
    b_got = after(b_got, a_sent)
    b_sum = [total(pick_f32(b, z, 0), b_got[:, :, z]) for z in range(4)]
    b_plus, b_minus, b_far = (t.astype(BF16) for t in b_sum[1:])
    b_from_minus, b_from_plus, b_from_far = shift(b_plus, dz=1), shift(b_minus, dz=-1), shift(b_far, dz=2)
    a_got = after(a_got, b_plus, b_minus, b_far)

    def shard(t):
        return tuple(v.reshape(-1, hidden) for v in gelu_pair(t[0], t[1], bias_in))

    ua = shard(total(a_half[0], a_got))
    ub = shard(total(b_sum[0], b_from_minus, b_from_plus, b_from_far))
    na, nb = ua[0].shape[0], ub[0].shape[0]

    def packed(*blocks):
        return jnp.concatenate(blocks)

    def opened(value, *sizes):
        ends, at = [], 0
        for n in sizes[:-1]:
            at += n
            ends.append(at)
        return jnp.split(value, ends)

    four = (na, na, nb, nb)
    u = packed(*ua, *ub)
    held = lax.optimization_barrier((*pieces_a, *pieces_b, u))
    pieces_a, pieces_b, u = held[:5], held[5:8], held[8]
    minus1, plus1, y1 = shift(u, dz=1), shift(u, dz=-1), shift(u, far=True)
    ma0, ma1, mb0, mb1 = opened(minus1, *four)
    pa0, pa1, pb0, pb1 = opened(plus1, *four)
    ya0, ya1, yb0, yb1 = opened(y1, *four)
    minus2 = shift(packed(ya0, ya1, ma0, mb0), dz=1)
    plus2 = shift(packed(ya0, ya1, pa1, pb1), dz=-1)
    y2 = shift(packed(pb0, pb1, mb0, mb1), far=True)
    mya0, mya1, fa0, fb0 = opened(minus2, na, na, na, nb)
    pya0, pya1, fa1, fb1 = opened(plus2, na, na, na, nb)
    ypb0, ypb1, ymb0, ymb1 = opened(y2, nb, nb, nb, nb)
    minus3, plus3 = shift(mya0, dz=1), shift(pya1, dz=-1)
    y3 = shift(packed(fb0, fb1), far=True)

    early = [
        (*ua, 0, 0, 0), (*ub, 1, 0, 0),
        (ma0, ma1, 0, 2, 0), (mb0, mb1, 1, 2, 0), (pa0, pa1, 0, 1, 0), (pb0, pb1, 1, 1, 0),
        (ya0, ya1, 0, 0, 1), (yb0, yb1, 1, 0, 1),
        (mya0, mya1, 0, 2, 1), (pya0, pya1, 0, 1, 1), (fa0, fa1, 0, 3, 0), (fb0, fb1, 1, 3, 0),
        (ypb0, ypb1, 1, 1, 1), (ymb0, ymb1, 1, 2, 1),
    ]
    late = [(minus3, plus3, 0, 3, 1), (*opened(y3, nb, nb), 1, 3, 1)]

    def both_cores(*rounds):
        act, pre = [], []
        for blocks in rounds:
            act.append(packed(*[b[0] for b in blocks]))
            pre.append(packed(*[b[1] for b in blocks]))
        swap = [swapped(packed(a, p)) for a, p in zip(act, pre)]
        act += [s[: s.shape[0] // 2] for s in swap]
        pre += [s[s.shape[0] // 2 :] for s in swap]
        return packed(*act), packed(*pre)

    act_early, pre_early = both_cores(early[:8], early[8:])
    act_late, pre_late = both_cores(late)
    places_early, places_late = ([(core, *b[2:]) for core in (0, 1) for b in part] for part in (early, late))

    def matching(array):
        parts = [jnp.stack([p[array].reshape(2, 4, 2, 8, -1) for p in pieces]) for pieces in (pieces_a, pieces_b)]
        return jnp.concatenate([parts[n][:, c, z, y].reshape(-1, parts[n].shape[-1]) for c, n, z, y in places_early + places_late])

    x_all, g_all = matching(0), matching(1)
    pre = packed(pre_early, pre_late)
    back = contract(pre, w_in, 1, 1).astype(BF16)
    found, at = {}, 0
    for place_of in places_early + places_late:
        n = (na, nb)[place_of[1]]
        found[place_of] = back[at : at + n].reshape(n // 8, 8, -1)
        at += n
    by_owner = []
    for part in (0, 1):
        slots = [found[core, part, z, y] for core in (0, 1) for z in range(4) for y in (0, 1)]
        v = jnp.stack(slots, axis=1)
        by_owner += [v[i].reshape(128, -1) for i in range(v.shape[0])]
    own_b, plus_b, minus_b, far_b, other_b, oplus_b, ominus_b, ofar_b = by_owner
    row = lax.axis_index("row")
    here = jnp.stack([own_b, plus_b, far_b, minus_b])
    there = jnp.stack([other_b, oplus_b, ofar_b, ominus_b])
    upper = row >= 4
    planes = (jnp.where(upper, there, here), jnp.where(upper, here, there))
    x_at = (4 - row % 4) % 4
    turned = [lax.dynamic_slice_in_dim(jnp.concatenate([p, p]), x_at, 4, 0) for p in planes]
    turned = jnp.concatenate(turned)
    arrived = lax.all_to_all(turned, "row", split_axis=0, concat_axis=0, tiled=True)
    act = packed(act_early, act_late)
    grad_w_out = contract(act, g_all, 0, 0).astype(BF16)
    grad_w_in = contract(x_all, pre, 0, 0).astype(BF16)
    portion = hidden // lax.axis_size("col")
    mine = lax.dynamic_slice_in_dim(after(pre, turned), lax.axis_index("col") * portion, portion, 1)
    grad_bias = jnp.sum(mine.astype(F32), axis=0)
    grad_in = contract(order, arrived.astype(F32).sum(axis=0).astype(BF16), 0, 0).astype(BF16)
    return grad_in, grad_w_in, grad_w_out, grad_bias


def solution(mesh):
    return jax.shard_map(
        local,
        mesh=mesh,
        in_specs=(P("row", "col"), P("row", "col"), P("col", "row"), P("row"), P("row", "col")),
        out_specs=(P("row", "col"), P("col", "row"), P("row", "col"), P(("row", "col"))),
        check_vma=False,
    )
```

```python
import jax
import jax.numpy as jnp
from jax import lax
from jax.sharding import PartitionSpec as P

coeff = 0.7978845608028654
AXES = ("row", "col")
F32, BF16 = jnp.float32, jnp.bfloat16


def place(y, x, z, core):
    y, x, z = y % 4, x % 4, z % 4
    return ((y % 2) * 4 + x) * 16 + ((y // 2) * 4 + z) * 2 + core


def shift(value, dx=0, dz=0, pair=False, far=False, swap=False):
    table = []
    for y in range(4):
        for x in range(4):
            for z in range(4):
                for k in range(2):
                    to_y = y ^ 1 if pair else y + 2 if far else y
                    table.append((place(y, x, z, k), place(to_y, x + dx, z + dz, k ^ 1 if swap else k)))
    return lax.ppermute(value, AXES, table)


def gelu_pair(preact, grad_act, bias):
    shifted = preact + bias
    tangent = jnp.tanh(coeff * (shifted + 0.044715 * shifted * shifted * shifted))
    activated = 0.5 * shifted * (1.0 + tangent)
    slope = 0.5 * (1.0 + tangent) + 0.5 * shifted * (1.0 - tangent * tangent) * coeff * (
        1.0 + 3.0 * 0.044715 * shifted * shifted
    )
    return activated.astype(BF16), (grad_act * slope).astype(BF16)


def contract(left, right, left_dim, right_dim):
    return lax.dot_general(left, right, (((left_dim,), (right_dim,)), ((), ())), preferred_element_type=F32)


def add(*terms):
    return sum(t.astype(F32) for t in terms).astype(BF16)


def relative_rows():
    col = lax.axis_index("col")
    core, z, y_hi = col % 2, (col // 2) % 4, col // 8
    row = jnp.arange(128, dtype=jnp.int32)[:, None]
    slot = row // 8
    d_core, d_z, d_y = slot // 8, (slot // 2) % 4, slot % 2
    d_z = jnp.where(d_z == 2, 3, jnp.where(d_z == 3, 2, d_z))
    source = ((jnp.bitwise_xor(y_hi, d_y) * 4 + (z + d_z) % 4) * 2 + jnp.bitwise_xor(core, d_core)) * 8 + row % 8
    return (source == jnp.arange(128, dtype=jnp.int32)[None, :]).astype(BF16)


def after(value, *earlier):
    return lax.optimization_barrier((value, *earlier))[0]


def total(*terms):
    return sum(t.astype(F32) for t in terms)


def swapped(value):
    return shift(value, swap=True)


def local(inputs, grad_out, w_in, bias_in, w_out):
    hidden = w_in.shape[1]
    order = relative_rows()

    own = jnp.stack([contract(order, a, 1, 0).astype(BF16) for a in (inputs, grad_out)])
    plus, minus, other = shift(own, dx=-1), shift(own, dx=1), shift(own, pair=True)
    far = jnp.stack([shift(minus[0], dx=1), shift(plus[1], dx=-1)])
    other_plus, other_minus = shift(other, dx=-1), shift(other, dx=1)
    other_far = shift(far, pair=True)
    pieces_a = [own, plus, minus, far, other]
    pieces_b = [other_plus, other_minus, other_far]

    def rows(pieces, array, core):
        return jnp.concatenate([p.reshape(2, 2, 64, -1)[array, core] for p in pieces])

    def pair_sums(pieces):
        m = len(pieces)
        sums = []
        for i, w, dim in ((0, w_in, 0), (1, w_out, 1)):
            both = contract(jnp.concatenate([rows(pieces, i, 0), rows(pieces, i, 1)]), w, 1, dim).astype(BF16)
            got = swapped(both[m * 64 :])
            sums.append((both[: m * 64].reshape(m, 4, 2, 8, hidden), got.reshape(m, 4, 2, 8, hidden)))
        return sums

    def pick(sums, *at):
        return jnp.stack([add(k[(slice(None), *at)], g[(slice(None), *at)]) for k, g in sums])

    def pick_f32(sums, *at):
        return jnp.stack([total(k[(slice(None), *at)], g[(slice(None), *at)]) for k, g in sums])

    a = pair_sums(pieces_a)
    a_far0, a_far1 = pick(a, 3, 0), pick(a, 3, 1)
    a_via_plus, a_via_minus = shift(a_far0, dz=1), shift(a_far1, dz=-1)
    pieces_b = list(lax.optimization_barrier((*pieces_b, a_far0, a_far1))[:3])
    b = pair_sums(pieces_b)
    a_plus = jnp.stack([add(pick_f32(a, 1, 0), a_via_plus), pick(a, 1, 1)])
    a_minus = jnp.stack([pick(a, 2, 0), add(pick_f32(a, 2, 1), a_via_minus)])
    a_from_minus, a_from_plus = shift(a_plus, dz=1), shift(a_minus, dz=-1)
    b_got = shift(after(pick(b, slice(None), 1), a_via_plus, a_via_minus), far=True)
    a_half = [total(pick_f32(a, 0, y), a_from_minus[y], a_from_plus[y]) for y in (0, 1)]
    a_sent = a_half[1].astype(BF16)
    a_got = shift(a_sent, far=True)
    b_got = after(b_got, a_sent)
    b_sum = [total(pick_f32(b, z, 0), b_got[:, :, z]) for z in range(4)]
    b_plus, b_minus, b_far = (t.astype(BF16) for t in b_sum[1:])
    b_from_minus, b_from_plus, b_from_far = shift(b_plus, dz=1), shift(b_minus, dz=-1), shift(b_far, dz=2)
    a_got = after(a_got, b_plus, b_minus, b_far)

    def shard(t):
        return tuple(v.reshape(-1, hidden) for v in gelu_pair(t[0], t[1], bias_in))

    ua = shard(total(a_half[0], a_got))
    ub = shard(total(b_sum[0], b_from_minus, b_from_plus, b_from_far))
    na, nb = ua[0].shape[0], ub[0].shape[0]

    def packed(*blocks):
        return jnp.concatenate(blocks)

    def opened(value, *sizes):
        ends, at = [], 0
        for n in sizes[:-1]:
            at += n
            ends.append(at)
        return jnp.split(value, ends)

    four = (na, na, nb, nb)
    u = packed(*ua, *ub)
    held = lax.optimization_barrier((*pieces_a, *pieces_b, u))
    pieces_a, pieces_b, u = held[:5], held[5:8], held[8]
    minus1, plus1, y1 = shift(u, dz=1), shift(u, dz=-1), shift(u, far=True)
    ma0, ma1, mb0, mb1 = opened(minus1, *four)
    pa0, pa1, pb0, pb1 = opened(plus1, *four)
    ya0, ya1, yb0, yb1 = opened(y1, *four)
    to_minus2, to_plus2 = packed(ya0, ya1, ma0, mb0), packed(ya0, ya1, pa1, pb1)
    minus2, plus2 = shift(to_minus2, dz=1), shift(to_plus2, dz=-1)
    y2 = shift(after(packed(pb0, pb1, mb0, mb1), to_minus2, to_plus2), far=True)
    mya0, mya1, fa0, fb0 = opened(minus2, na, na, na, nb)
    pya0, pya1, fa1, fb1 = opened(plus2, na, na, na, nb)
    ypb0, ypb1, ymb0, ymb1 = opened(y2, nb, nb, nb, nb)
    minus3, plus3 = shift(mya0, dz=1), shift(pya1, dz=-1)
    y3 = shift(packed(fb0, fb1), far=True)

    early = [
        (*ua, 0, 0, 0), (*ub, 1, 0, 0),
        (ma0, ma1, 0, 2, 0), (mb0, mb1, 1, 2, 0), (pa0, pa1, 0, 1, 0), (pb0, pb1, 1, 1, 0),
        (ya0, ya1, 0, 0, 1), (yb0, yb1, 1, 0, 1),
        (mya0, mya1, 0, 2, 1), (pya0, pya1, 0, 1, 1), (fa0, fa1, 0, 3, 0), (fb0, fb1, 1, 3, 0),
        (ypb0, ypb1, 1, 1, 1), (ymb0, ymb1, 1, 2, 1),
    ]
    late = [(minus3, plus3, 0, 3, 1), (*opened(y3, nb, nb), 1, 3, 1)]

    def both_cores(*rounds):
        act, pre = [], []
        for blocks in rounds:
            act.append(packed(*[b[0] for b in blocks]))
            pre.append(packed(*[b[1] for b in blocks]))
        swap = [swapped(packed(a, p)) for a, p in zip(act, pre)]
        act += [s[: s.shape[0] // 2] for s in swap]
        pre += [s[s.shape[0] // 2 :] for s in swap]
        return packed(*act), packed(*pre)

    act_early, pre_early = both_cores(early[:8], early[8:])
    act_late, pre_late = both_cores(late)
    places_early, places_late = ([(core, *b[2:]) for core in (0, 1) for b in part] for part in (early, late))

    def matching(array):
        parts = [jnp.stack([p[array].reshape(2, 4, 2, 8, -1) for p in pieces]) for pieces in (pieces_a, pieces_b)]
        return jnp.concatenate([parts[n][:, c, z, y].reshape(-1, parts[n].shape[-1]) for c, n, z, y in places_early + places_late])

    x_all, g_all = matching(0), matching(1)
    pre = packed(pre_early, pre_late)
    back = contract(pre, w_in, 1, 1).astype(BF16)
    found, at = {}, 0
    for place_of in places_early + places_late:
        n = (na, nb)[place_of[1]]
        found[place_of] = back[at : at + n].reshape(n // 8, 8, -1)
        at += n
    by_owner = []
    for part in (0, 1):
        slots = [found[core, part, z, y] for core in (0, 1) for z in range(4) for y in (0, 1)]
        v = jnp.stack(slots, axis=1)
        by_owner += [v[i].reshape(128, -1) for i in range(v.shape[0])]
    own_b, plus_b, minus_b, far_b, other_b, oplus_b, ominus_b, ofar_b = by_owner
    row = lax.axis_index("row")
    here = jnp.stack([own_b, plus_b, far_b, minus_b])
    there = jnp.stack([other_b, oplus_b, ofar_b, ominus_b])
    upper = row >= 4
    planes = (jnp.where(upper, there, here), jnp.where(upper, here, there))
    x_at = (4 - row % 4) % 4
    turned = [lax.dynamic_slice_in_dim(jnp.concatenate([p, p]), x_at, 4, 0) for p in planes]
    turned = jnp.concatenate(turned)
    arrived = lax.all_to_all(turned, "row", split_axis=0, concat_axis=0, tiled=True)
    act = packed(act_early, act_late)
    grad_w_out = contract(act, g_all, 0, 0).astype(BF16)
    grad_w_in = contract(x_all, pre, 0, 0).astype(BF16)
    portion = hidden // lax.axis_size("col")
    mine = lax.dynamic_slice_in_dim(after(pre, turned), lax.axis_index("col") * portion, portion, 1)
    grad_bias = jnp.sum(mine.astype(F32), axis=0)
    grad_in = contract(order, arrived.astype(F32).sum(axis=0).astype(BF16), 0, 0).astype(BF16)
    return grad_in, grad_w_in, grad_w_out, grad_bias


def solution(mesh):
    return jax.shard_map(
        local,
        mesh=mesh,
        in_specs=(P("row", "col"), P("row", "col"), P("col", "row"), P("row"), P("row", "col")),
        out_specs=(P("row", "col"), P("col", "row"), P("row", "col"), P(("row", "col"))),
        check_vma=False,
    )
```
